256 devices in a mesh: dp: 4 (over y), space: 64 (over z, x, core).
Axes of the slice: x: 4, y: 4, z: 8, core: 2. Of those that a mesh axis runs over, the one named last changes fastest.
Arguments:
- features: bfloat16 [4, 128, 8, 8, 8, 128], P('dp', 'space'), may hold values from -6 to 6
- occupancy: int32 [4, 128, 8, 8, 8], P('dp', 'space'), may hold values from 0 to 1
- neighbours: int32 [4, 128, 26], P('dp', 'space'), may hold values from -1 to 127, as said below
- weight: bfloat16 [27, 128, 128], replicated, may hold values from -0.109375 to 0.109375
- cotangent: bfloat16 [4, 128, 8, 8, 8, 128], P('dp', 'space'), may hold values from -6 to 6
Outputs:
- response: bfloat16 [4, 128, 8, 8, 8, 128], P('dp', 'space')
- grad_input: bfloat16 [4, 128, 8, 8, 8, 128], P('dp', 'space')
- grad_weight: float32 [3456, 128], P('space')
The draws below stay inside these ranges and needn't reach their ends.
Inputs may be any that keep to these rules, and one draw needn't show every extreme that they name: `neighbours`: A scan's blocks sit in a coarse grid of 64 slabs along the first dimension, each one cell thick and 4 cells across; each slab holds exactly 2 blocks, numbered slab by slab and inside a slab in the Morton order of their cells, so block g lies in slab g // 2; entry o of block g names the block in the adjacent cell in direction o, or -1 if that cell is empty or outside the grid; the relation is symmetric.
All inputs are finite; a program needn't handle non-finite values.
Results may differ from the reference program's by a relative error of at most 0.001.
Values may be sent and summed in bfloat16 or wider, within the bound.
A program may use at most 64 MiB of HBM per device.

```python
import math
import jax
import jax.numpy as jnp
from jax import lax

C = 128
BLOCK = 8
BLOCKS_DEV = 2
SCANS = 4
CELLS = 4
BLOCKS = 128
N_SPACE = 64


directions = [(along_x, along_y, along_z) for along_x in (-1, 0, 1) for along_y in (-1, 0, 1) for along_z in (-1, 0, 1) if (along_x, along_y, along_z) != (0, 0, 0)]


def split_code(codes, total_bits):
    coords = [jnp.zeros_like(codes) for axis_number in range(2)]
    for position in range(total_bits):
        bit_value = codes >> position & 1
        coords[position % 2] = coords[position % 2] + (bit_value << position // 2)
    return coords


def join_code(coords, total_bits):
    codes = jnp.zeros_like(coords[0])
    for position in range(total_bits):
        bit_value = coords[position % 2] >> position // 2 & 1
        codes = codes + (bit_value << position)
    return codes


def one_scan(key):
    total_bits = CELLS.bit_length() - 1
    extents = [2 ** len([position for position in range(total_bits) if position % 2 == axis_number]) for axis_number in range(2)]
    cell_ids = jnp.arange(CELLS, dtype=jnp.int32)
    scores = jax.random.randint(key, (N_SPACE, CELLS), 0, 1 << 20, dtype=jnp.int32) * CELLS + cell_ids[None, :]
    picked = jnp.sort(jnp.argsort(scores, axis=1)[:, :BLOCKS_DEV].astype(jnp.int32), axis=1)
    slab_ids = jnp.arange(N_SPACE, dtype=jnp.int32)
    numbers = slab_ids[:, None] * BLOCKS_DEV + jnp.arange(BLOCKS_DEV, dtype=jnp.int32)[None, :]
    owner = jnp.full((N_SPACE, CELLS), -1, jnp.int32).at[jnp.broadcast_to(slab_ids[:, None], picked.shape), picked].set(numbers)
    coords = split_code(picked, total_bits)
    slabs = jnp.broadcast_to(slab_ids[:, None], picked.shape)
    columns = []
    for offset in directions:
        slab_to = slabs + offset[0]
        moved_y = coords[0] + offset[1]
        moved_z = coords[1] + offset[2]
        inside = (slab_to >= 0) & (slab_to < N_SPACE) & (moved_y >= 0) & (moved_y < extents[0]) & (moved_z >= 0) & (moved_z < extents[1])
        clipped_code = join_code([jnp.clip(moved_y, 0, extents[0] - 1), jnp.clip(moved_z, 0, extents[1] - 1)], total_bits)
        target = owner[jnp.clip(slab_to, 0, N_SPACE - 1), clipped_code]
        columns.append(jnp.where(inside, target, -1))
    return jnp.stack(columns, axis=-1).reshape(BLOCKS, 26).astype(jnp.int32)


def draw_neighbours(key, part):
    tables = [one_scan(jax.random.fold_in(key, 100 + scan_number)) for scan_number in range(SCANS)]
    return jnp.stack(tables).astype(jnp.int32)


def draw_occupancy(key, part):
    rate_key = jax.random.fold_in(key, 7)
    voxel_key = jax.random.fold_in(key, 11)
    rates = jax.random.randint(rate_key, (SCANS, BLOCKS, 1, 1, 1), 1, 9, dtype=jnp.int32)
    voxels = jax.random.randint(voxel_key, (SCANS, BLOCKS, BLOCK, BLOCK, BLOCK), 0, 8, dtype=jnp.int32)
    return (voxels < rates).astype(jnp.int32)


def block_scale(own_key, dims, shards, smallest, largest):
    loudness = 1.0
    for dim, parts in shards:
        steps = jax.random.uniform(jax.random.fold_in(jax.random.fold_in(own_key, 6), dim), (parts,), jnp.float32, smallest / len(shards), largest / len(shards))
        loudness = loudness * jnp.repeat(jnp.exp(steps), dims[dim] // parts).reshape((-1,) + (1,) * (len(dims) - 1 - dim))
    return loudness


def noise(key, shape, width, most, cuts=(), held_as=jnp.bfloat16):
    loudness = block_scale(key, shape, cuts, -0.22, 0.18) if cuts else 1.0
    entries = jax.random.normal(key, shape, jnp.float32) * width * loudness
    return jnp.minimum(jnp.maximum(entries, -most), most).astype(held_as)


def setup_inputs(seed: int = 0) -> dict:
    key_of = jax.random.split(jax.random.key(seed), 6)
    return {
        "features": noise(key_of[0], (SCANS, BLOCKS, BLOCK, BLOCK, BLOCK, C), 1.0, 6.0, ((0, 4), (1, 64))),
        "occupancy": draw_occupancy(jax.random.fold_in(key_of[5], 71), 0),
        "neighbours": draw_neighbours(jax.random.fold_in(key_of[5], 71), 0),
        "weight": noise(key_of[3], (27, C, C), (27 * C) ** -0.5, 0.109375),
        "cotangent": noise(key_of[4], (SCANS, BLOCKS, BLOCK, BLOCK, BLOCK, C), 1.0, 6.0, ((0, 4), (1, 64))),
    }


directions = [(along_x, along_y, along_z) for along_x in (-1, 0, 1) for along_y in (-1, 0, 1) for along_z in (-1, 0, 1) if (along_x, along_y, along_z) != (0, 0, 0)]
kernel_taps = [(along_x, along_y, along_z) for along_x in range(3) for along_y in range(3) for along_z in range(3)]

def side_slices(offset, extent):
    chosen = []
    for stride in offset:
        if stride == 1:
            chosen.append(slice(extent - 1, extent))
        elif stride == -1:
            chosen.append(slice(0, 1))
        else:
            chosen.append(slice(0, extent))
    return tuple(chosen)

def rim_slices(offset, extent):
    chosen = []
    for stride in offset:
        if stride == 1:
            chosen.append(slice(extent + 1, extent + 2))
        elif stride == -1:
            chosen.append(slice(0, 1))
        else:
            chosen.append(slice(1, extent + 1))
    return tuple(chosen)

def reference(features, occupancy, neighbours, weight, cotangent):
    total_blocks = SCANS * BLOCKS
    active = (occupancy > 0).reshape(total_blocks, BLOCK, BLOCK, BLOCK, 1)
    zero_bf = jnp.zeros((), jnp.bfloat16)
    masked = jnp.where(active, features.reshape(total_blocks, BLOCK, BLOCK, BLOCK, C), zero_bf)
    upstream = jnp.where(active, cotangent.reshape(total_blocks, BLOCK, BLOCK, BLOCK, C), zero_bf)
    links = neighbours.reshape(total_blocks, 26).astype(jnp.int32)

    def padded_of(field, number):
        own = lax.dynamic_index_in_dim(field, number, 0, keepdims=False)
        padded = jnp.pad(own, ((1, 1), (1, 1), (1, 1), (0, 0)))
        scan_base = number // BLOCKS * BLOCKS
        for slot_index, offset in enumerate(directions):
            other = links[number, slot_index]
            source_block = lax.dynamic_index_in_dim(field, (scan_base + jnp.maximum(other, 0)).astype(jnp.int32), 0, keepdims=False)
            opposite = tuple((-stride for stride in offset))
            portion = source_block[side_slices(opposite, BLOCK)]
            portion = jnp.where(other >= 0, portion, zero_bf)
            padded = padded.at[rim_slices(offset, BLOCK)].set(portion)
        return padded

    def visit(carry, number):
        padded_x = padded_of(masked, number)
        padded_g = padded_of(upstream, number)
        own_g = lax.dynamic_index_in_dim(upstream, number, 0, keepdims=False).reshape(-1, C)
        own_active = lax.dynamic_index_in_dim(active, number, 0, keepdims=False)
        forward_sum = jnp.zeros((BLOCK ** 3, C), jnp.float32)
        backward_sum = jnp.zeros((BLOCK ** 3, C), jnp.float32)
        grads = []
        for tap_index, (along_x, along_y, along_z) in enumerate(kernel_taps):
            window = padded_x[along_x:along_x + BLOCK, along_y:along_y + BLOCK, along_z:along_z + BLOCK].reshape(-1, C)
            forward_sum = forward_sum + jnp.dot(window, weight[tap_index], preferred_element_type=jnp.float32)
            gwindow = padded_g[2 - along_x:2 - along_x + BLOCK, 2 - along_y:2 - along_y + BLOCK, 2 - along_z:2 - along_z + BLOCK].reshape(-1, C)
            backward_sum = backward_sum + jnp.dot(gwindow, weight[tap_index].T, preferred_element_type=jnp.float32)
            grads.append(jnp.dot(window.T, own_g, preferred_element_type=jnp.float32))
        carry = carry + jnp.concatenate(grads, axis=0)
        response_block = jnp.where(own_active, forward_sum.reshape(BLOCK, BLOCK, BLOCK, C), jnp.zeros((), jnp.float32)).astype(jnp.bfloat16)
        grad_block = jnp.where(own_active, backward_sum.reshape(BLOCK, BLOCK, BLOCK, C), jnp.zeros((), jnp.float32)).astype(jnp.bfloat16)
        return (carry, (response_block, grad_block))
    start = jnp.zeros((27 * C, C), jnp.float32)
    kernel, (responses, grads_in) = lax.scan(visit, start, jnp.arange(total_blocks, dtype=jnp.int32))
    scale_factor = 1.0 / math.sqrt(SCANS * BLOCKS * BLOCK ** 3)
    response = responses.reshape(SCANS, BLOCKS, BLOCK, BLOCK, BLOCK, C)
    grad_input = grads_in.reshape(SCANS, BLOCKS, BLOCK, BLOCK, BLOCK, C)
    return (response, grad_input, kernel * scale_factor)
```

```python
import functools
import math

import jax
import jax.numpy as jnp
from jax import lax
from jax.experimental import pallas as pl
from jax.experimental.pallas import tpu as pltpu
from jax.sharding import PartitionSpec as P

MESH = pl.DeviceIdType.MESH
BF = jnp.bfloat16
F32 = jnp.float32
ROWS = 54
PART = 16
CHUNKS = ((3, 2), (0, 3), (5, 3))
TX_ORDER = (1, 0, 2)


def slot_of(dx, dy, dz):
    number = 9 * (dx + 1) + 3 * (dy + 1) + (dz + 1)
    return number if number < 13 else number - 1


def kernel(
    x_hbm, g_hbm, occ_hbm, links, w_hbm,
    resp_hbm, gin_hbm, gw_ref,
    xv, gv, occv, wv, wt, mask, xm, gm, gmb, gt, xs, gs,
    halo_out, halo_in, cbuf, csnd, crcv, xyb, own, rxy, zp, rz, fin, outv,
    in_sem, out_sem, halo_s, halo_r, core_s, core_r, xy_s, xy_r, z_s, z_r, y_s, y_r,
):
    me_y = lax.axis_index("dp")
    me_s = lax.axis_index("space")
    me_c = lax.rem(me_s, 2)
    me_x = lax.rem(me_s // 2, 4)
    me_z = me_s // 8
    other_c = 1 - me_c

    def at(y, z, x, c):
        return (y, (z * 4 + x) * 2 + c)

    after = (me_y, lax.rem(me_s + 1, 64))
    before = (me_y, lax.rem(me_s + 63, 64))
    partner = at(me_y, me_z, me_x, other_c)

    def xy_peer(k):
        return lax.rem(me_x + k // 4, 4), lax.rem(me_y + lax.rem(k, 4), 4)

    loads = [
        pltpu.make_async_copy(src, dst, in_sem.at[i])
        for i, (src, dst) in enumerate(
            ((occ_hbm, occv), (x_hbm, xv), (g_hbm, gv), (w_hbm, wv))
        )
    ]
    for load in loads:
        load.start()

    barrier = pltpu.get_barrier_semaphore()

    def greet(device):
        pl.semaphore_signal(barrier, inc=1, device_id=device, device_id_type=MESH)

    greet(before)
    greet(after)
    greet(partner)

    def greet_xy(k, carry):
        px, py = xy_peer(k)
        greet(at(py, me_z, px, me_c))
        return carry

    lax.fori_loop(1, 16, greet_xy, 0)

    def greet_z(k, carry):
        greet(at(me_y, lax.rem(me_z + k, 8), me_x, me_c))
        return carry

    lax.fori_loop(1, 8, greet_z, 0)

    for load in loads[:3]:
        load.wait()

    eye = (
        lax.broadcasted_iota(jnp.int32, (8, 8, 8), 1)
        == lax.broadcasted_iota(jnp.int32, (8, 8, 8), 2)
    )
    ones = jnp.ones((8, 128), F32)

    def mask_plane(i, carry):
        occ = occv[i // 8, lax.rem(i, 8)]
        spread = jnp.broadcast_to(occ[:, None, :], (8, 8, 8))
        picked = jnp.where(eye & (spread > 0), 1.0, 0.0).astype(F32).reshape(64, 8)
        m = jnp.dot(picked, ones, preferred_element_type=F32)
        mask[i] = m
        keep = m > 0.5
        xk = jnp.where(keep, xv[i].astype(F32), 0.0)
        gk = jnp.where(keep, gv[i].astype(F32), 0.0)
        xm[i] = xk.reshape(8, 8, 128)
        gm[i] = gk.reshape(8, 8, 128)
        gmb[i] = gk.astype(BF)
        return carry

    lax.fori_loop(0, 16, mask_plane, 0)

    for t, src in enumerate((xm, gm)):
        for side in range(2):
            for b in range(2):
                halo_out[t, side, b] = src[8 * b + 7 * side].reshape(64, 128).astype(BF)

    pl.semaphore_wait(barrier, 25)

    def halo_copy(t, side):
        return pltpu.make_async_remote_copy(
            src_ref=halo_out.at[t, side],
            dst_ref=halo_in.at[t, 1 - side],
            send_sem=halo_s.at[t, side],
            recv_sem=halo_r.at[t, 1 - side],
            device_id=after if side == 1 else before,
            device_id_type=MESH,
        )

    halos = [[halo_copy(t, side) for side in range(2)] for t in range(2)]
    for t in range(2):
        for side in range(2):
            halos[t][side].start()

    zi = lax.broadcasted_iota(jnp.int32, (10, 8, 128), 1)

    def weights_of(b, dx, local):
        wanted = (me_s + dx) * 2 + local

        def one(dy, dz):
            link = links[b, slot_of(dx, dy, dz)]
            return jnp.where((link == wanted) & (link >= 0), 1.0, 0.0).astype(F32)

        return one

    def put_plane(dst, index, centre, low, high):
        shifted = (
            pltpu.roll(jnp.where(zi == 7, low, centre), 1, 1),
            centre,
            pltpu.roll(jnp.where(zi == 0, high, centre), 7, 1),
        )
        for ty in range(3):
            for tz in range(3):
                col = (3 * ty + tz) * 128
                dst[index, :, col : col + 128] = (
                    shifted[tz][ty : ty + 8].reshape(64, 128).astype(BF)
                )

    def own_planes(src, dst):
        for b in range(2):
            one = weights_of(b, 0, 1 - b)
            w = {
                (dy, dz): one(dy, dz)
                for dy in (-1, 0, 1)
                for dz in (-1, 0, 1)
                if (dy, dz) != (0, 0)
            }

            def plane(p, carry, b=b, w=w):
                mine = src[8 * b + p]
                theirs = src[8 * (1 - b) + p]
                first, last = theirs[0:1], theirs[7:8]

                def zone(dz):
                    middle = mine if dz == 0 else theirs * w[0, dz]
                    return jnp.concatenate(
                        [last * w[-1, dz], middle, first * w[1, dz]], axis=0
                    )

                put_plane(dst, 10 * b + p + 1, zone(0), zone(-1), zone(1))
                return carry

            lax.fori_loop(0, 8, plane, 0)

    def rim_planes(t, dst):
        for side, dx in ((0, -1), (1, 1)):
            p0 = halo_in[t, side, 0].astype(F32).reshape(8, 8, 128)
            p1 = halo_in[t, side, 1].astype(F32).reshape(8, 8, 128)
            for b in range(2):
                w0 = weights_of(b, dx, 0)
                w1 = weights_of(b, dx, 1)

                def zone(dz):
                    def mix(dy, rows):
                        return p0[rows] * w0(dy, dz) + p1[rows] * w1(dy, dz)

                    return jnp.concatenate(
                        [mix(-1, slice(7, 8)), mix(0, slice(0, 8)), mix(1, slice(0, 1))],
                        axis=0,
                    )

                put_plane(dst, 10 * b + 9 * side, zone(0), zone(-1), zone(1))

    def kernel_grad(tx):
        for ty in range(3):
            total = None
            for b in range(2):
                window = xs[10 * b + tx : 10 * b + tx + 8, :, 384 * ty : 384 * ty + 384]
                part = jnp.dot(
                    gt[:, 512 * b : 512 * b + 512],
                    window.reshape(512, 384),
                    preferred_element_type=F32,
                )
                total = part if total is None else total + part
            for tz in range(3):
                tap = 9 * tx + 3 * ty + tz
                cbuf[128 * tap : 128 * tap + 128, :] = total[:, 128 * tz : 128 * tz + 128].T

    def core_copy(n):
        z0, nz = CHUNKS[n]
        return pltpu.make_async_remote_copy(
            src_ref=csnd.at[pl.ds(4 * z0, 4 * nz)],
            dst_ref=crcv.at[pl.ds(4 * z0, 4 * nz)],
            send_sem=core_s.at[n],
            recv_sem=core_r.at[n],
            device_id=partner,
            device_id_type=MESH,
        )

    def core_send(n):
        z0, nz = CHUNKS[n]

        def fill(j, carry):
            csnd[j] = cbuf[pl.ds(ROWS * (2 * j + other_c), 64), :]
            return carry

        lax.fori_loop(4 * z0, 4 * (z0 + nz), fill, 0)
        core_copy(n).start()

    def xy_copy(n, k):
        z0, nz = CHUNKS[n]
        px, py = xy_peer(k)
        return pltpu.make_async_remote_copy(
            src_ref=xyb.at[px, py, pl.ds(z0, nz)],
            dst_ref=rxy.at[k - 1, pl.ds(z0, nz)],
            send_sem=xy_s.at[n, k - 1],
            recv_sem=xy_r.at[n, k - 1],
            device_id=at(py, me_z, px, me_c),
            device_id_type=MESH,
        )

    def xy_send(n):
        z0, nz = CHUNKS[n]
        core_copy(n).wait()

        def fill(j, carry):
            summed = cbuf[pl.ds(ROWS * (2 * j + me_c), 64), :] + crcv[j]
            for q in range(4):
                xyb[lax.rem(j, 4), q, j // 4] = summed[PART * q : PART * q + PART]
            return carry

        lax.fori_loop(4 * z0, 4 * (z0 + nz), fill, 0)

        def go(k, carry):
            xy_copy(n, k).start()
            return carry

        lax.fori_loop(1, 16, go, 0)

        def keep(z, carry):
            j = 4 * z + me_x
            own[z] = (
                cbuf[pl.ds(ROWS * (2 * j + me_c) + PART * me_y, PART), :]
                + crcv[j, pl.ds(pl.multiple_of(PART * me_y, PART), PART), :]
            )
            return carry

        lax.fori_loop(z0, z0 + nz, keep, 0)

    def z_copy(slot, target):
        return pltpu.make_async_remote_copy(
            src_ref=zp.at[target],
            dst_ref=rz.at[slot],
            send_sem=z_s.at[target],
            recv_sem=z_r.at[slot],
            device_id=at(me_y, target, me_x, me_c),
            device_id_type=MESH,
        )

    def z_send(n):
        z0, nz = CHUNKS[n]

        def arrived(k, carry):
            xy_copy(n, k).wait()
            return carry

        lax.fori_loop(1, 16, arrived, 0)

        def add(z, carry):
            total = own[z]
            for k in range(15):
                total = total + rxy[k, z]
            zp[z] = total

            @pl.when(z != me_z)
            def _():
                z_copy(me_z, z).start()

            return carry

        lax.fori_loop(z0, z0 + nz, add, 0)

    def transposed_weights():
        def turn(t, carry):
            wt[26 - t] = wv[t].T
            return carry

        lax.fori_loop(0, 27, turn, 0)

    def product(shifts, taps, out_index, out_hbm, part):
        b = part // 2
        start = 10 * b + 4 * lax.rem(part, 2)
        total = None
        for tx in range(3):
            window = shifts[pl.ds(start + tx, 4)].reshape(256, 1152)
            piece = jnp.dot(
                window, taps[9 * tx : 9 * tx + 9].reshape(1152, 128),
                preferred_element_type=F32,
            )
            total = piece if total is None else total + piece
        planes = pl.ds(4 * part, 4)
        keep = mask[planes].reshape(256, 128) > 0.5
        outv[out_index, planes] = jnp.where(keep, total, 0.0).astype(BF).reshape(4, 64, 128)

    def products(shifts, taps, out_index, out_hbm, lo, hi):
        def one(part, carry):
            product(shifts, taps, out_index, out_hbm, part)
            return carry

        lax.fori_loop(lo, hi, one, 0)

    def out_copy(index):
        dst = (resp_hbm, gin_hbm)[index]
        return pltpu.make_async_copy(outv.at[index], dst, out_sem.at[index])

    own_planes(xm, xs)
    for k in range(8):
        gt[:, 128 * k : 128 * k + 128] = gmb[2 * k : 2 * k + 2].reshape(128, 128).T
    kernel_grad(1)
    core_send(0)
    halos[0][0].wait()
    halos[0][1].wait()
    rim_planes(0, xs)
    kernel_grad(0)
    core_send(1)
    xy_send(0)
    kernel_grad(2)
    core_send(2)
    xy_send(1)
    own_planes(gm, gs)
    xy_send(2)

    loads[3].wait()
    z_send(0)
    products(xs, wv, 0, resp_hbm, 0, 2)
    z_send(1)
    products(xs, wv, 0, resp_hbm, 2, 4)
    out_copy(0).start()
    z_send(2)
    halos[1][0].wait()
    halos[1][1].wait()
    rim_planes(1, gs)
    transposed_weights()
    products(gs, wt, 1, gin_hbm, 0, 2)

    def z_done(k, carry):
        source = lax.rem(me_z + k, 8)
        z_copy(source, source).wait_recv()
        z_copy(me_z, source).wait_send()
        return carry

    lax.fori_loop(1, 8, z_done, 0)
    rz[me_z] = zp[me_z]
    total = rz[0]
    for z in range(1, 8):
        total = total + rz[z]
    fin[me_y] = total * (1.0 / math.sqrt(4 * 128 * 8**3))

    def y_copy(slot, k):
        return pltpu.make_async_remote_copy(
            src_ref=fin.at[me_y],
            dst_ref=fin.at[slot],
            send_sem=y_s.at[k],
            recv_sem=y_r.at[slot],
            device_id=at(lax.rem(me_y + k, 4), me_z, me_x, me_c),
            device_id_type=MESH,
        )

    for k in range(1, 4):
        y_copy(me_y, k).start()
    products(gs, wt, 1, gin_hbm, 2, 4)
    out_copy(1).start()
    for k in range(1, 4):
        y_copy(lax.rem(me_y + k, 4), k).wait_recv()
        y_copy(me_y, k).wait_send()
    gw_ref[...] = fin[...].reshape(64, 128)[:ROWS]
    out_copy(0).wait()
    out_copy(1).wait()


def per_device(features, occupancy, neighbours, weight, cotangent):
    dma = pltpu.SemaphoreType.DMA
    anywhere = pl.BlockSpec(memory_space=pl.ANY)
    resp, gin, gw = pl.pallas_call(
        kernel,
        out_shape=(
            jax.ShapeDtypeStruct((16, 64, 128), BF),
            jax.ShapeDtypeStruct((16, 64, 128), BF),
            jax.ShapeDtypeStruct((ROWS, 128), F32),
        ),
        in_specs=[
            anywhere,
            anywhere,
            anywhere,
            pl.BlockSpec(memory_space=pltpu.SMEM),
            anywhere,
        ],
        out_specs=(anywhere, anywhere, pl.BlockSpec(memory_space=pltpu.VMEM)),
        scratch_shapes=[
            pltpu.VMEM((16, 64, 128), BF),
            pltpu.VMEM((16, 64, 128), BF),
            pltpu.VMEM((2, 8, 8, 8), jnp.int32),
            pltpu.VMEM((27, 128, 128), BF),
            pltpu.VMEM((27, 128, 128), BF),
            pltpu.VMEM((16, 64, 128), F32),
            pltpu.VMEM((16, 8, 8, 128), F32),
            pltpu.VMEM((16, 8, 8, 128), F32),
            pltpu.VMEM((16, 64, 128), BF),
            pltpu.VMEM((128, 1024), BF),
            pltpu.VMEM((20, 64, 1152), BF),
            pltpu.VMEM((20, 64, 1152), BF),
            pltpu.VMEM((2, 2, 2, 64, 128), BF),
            pltpu.VMEM((2, 2, 2, 64, 128), BF),
            pltpu.VMEM((3472, 128), F32),
            pltpu.VMEM((32, 64, 128), F32),
            pltpu.VMEM((32, 64, 128), F32),
            pltpu.VMEM((4, 4, 8, PART, 128), F32),
            pltpu.VMEM((8, PART, 128), F32),
            pltpu.VMEM((15, 8, PART, 128), F32),
            pltpu.VMEM((8, PART, 128), F32),
            pltpu.VMEM((8, PART, 128), F32),
            pltpu.VMEM((4, PART, 128), F32),
            pltpu.VMEM((2, 16, 64, 128), BF),
            dma((4,)),
            dma((2,)),
            dma((2, 2)),
            dma((2, 2)),
            dma((3,)),
            dma((3,)),
            dma((3, 15)),
            dma((3, 15)),
            dma((8,)),
            dma((8,)),
            dma((4,)),
            dma((4,)),
        ],
        compiler_params=pltpu.CompilerParams(collective_id=0, has_side_effects=True),
        name="sparse_conv_step",
    )(
        features.reshape(16, 64, 128),
        cotangent.reshape(16, 64, 128),
        occupancy[0],
        neighbours[0],
        weight,
    )
    shape = features.shape
    return resp.reshape(shape), gin.reshape(shape), gw


def solution(mesh):
    placed = (
        P("dp", "space", None, None, None, None),
        P("dp", "space", None, None, None),
        P("dp", "space", None),
        P(),
        P("dp", "space", None, None, None, None),
    )
    return jax.shard_map(
        per_device,
        mesh=mesh,
        in_specs=placed,
        out_specs=(
            P("dp", "space", None, None, None, None),
            P("dp", "space", None, None, None, None),
            P("space", None),
        ),
        check_vma=False,
    )
```

```python
import functools
import math

import jax
import jax.numpy as jnp
from jax import lax
from jax.experimental import pallas as pl
from jax.experimental.pallas import tpu as pltpu
from jax.sharding import PartitionSpec as P

MESH = pl.DeviceIdType.MESH
BF = jnp.bfloat16
F32 = jnp.float32
ROWS = 54
PART = 14
SLOT = 16
CHUNKS = ((3, 2), (0, 3), (5, 3))


def slot_of(dx, dy, dz):
    number = 9 * (dx + 1) + 3 * (dy + 1) + (dz + 1)
    return number if number < 13 else number - 1


def kernel(
    x_hbm, g_hbm, occ_hbm, links, w_hbm,
    resp_hbm, gin_hbm, gw_ref,
    xv, gv, occv, wv, wt, mask, xm, gm, gmb, gt, xs, gs,
    halo_x, halo_g, halo_o, cbuf, csnd, crcv, xyb, own, rxy, zp, rz, fin, outv,
    in_sem, out_sem, halo_s, halo_r, core_s, core_r, xy_s, xy_r, z_s, z_r, y_s, y_r, ready,
):
    me_y = lax.axis_index("dp")
    me_s = lax.axis_index("space")
    me_c = lax.rem(me_s, 2)
    me_x = lax.rem(me_s // 2, 4)
    me_z = me_s // 8
    other_c = 1 - me_c

    def at(y, z, x, c):
        return (y, (z * 4 + x) * 2 + c)

    after = (me_y, lax.rem(me_s + 1, 64))
    before = (me_y, lax.rem(me_s + 63, 64))
    partner = at(me_y, me_z, me_x, other_c)

    def xy_peer(k):
        return lax.rem(me_x + k // 4, 4), lax.rem(me_y + lax.rem(k, 4), 4)

    loads = [
        pltpu.make_async_copy(src, dst, in_sem.at[i])
        for i, (src, dst) in enumerate(
            ((occ_hbm, occv), (x_hbm, xv), (g_hbm, gv), (w_hbm, wv))
        )
    ]
    for load in loads:
        load.start()

    barrier = pltpu.get_barrier_semaphore()

    def greet(device):
        pl.semaphore_signal(barrier, inc=1, device_id=device, device_id_type=MESH)

    near = [
        at(me_y, me_z, lax.rem(me_x + d, 4), me_c) for d in (1, 3)
    ] + [
        at(lax.rem(me_y + d, 4), me_z, me_x, me_c) for d in (1, 3)
    ] + [
        at(me_y, lax.rem(me_z + d, 8), me_x, me_c) for d in (1, 7)
    ]
    for device in [before, after, partner] + near:
        greet(device)

    def round_signal(r):
        for device in near:
            pl.semaphore_signal(ready.at[r], inc=1, device_id=device, device_id_type=MESH)

    def round_wait(r):
        pl.semaphore_wait(ready.at[r], 6)

    pl.semaphore_wait(barrier, 9)

    def halo_copies(side):
        plane = 7 * side
        return [
            pltpu.make_async_remote_copy(
                src_ref=src.at[:, plane],
                dst_ref=dst.at[1 - side],
                send_sem=halo_s.at[t, side],
                recv_sem=halo_r.at[t, 1 - side],
                device_id=after if side == 1 else before,
                device_id_type=MESH,
            )
            for t, (src, dst) in enumerate(
                ((occ_hbm, halo_o), (x_hbm, halo_x), (g_hbm, halo_g))
            )
        ]

    halos = [halo_copies(0), halo_copies(1)]
    for t in range(3):
        for side in range(2):
            halos[side][t].start()
    round_signal(0)

    for load in loads[:3]:
        load.wait()

    eye = (
        lax.broadcasted_iota(jnp.int32, (8, 8, 8), 1)
        == lax.broadcasted_iota(jnp.int32, (8, 8, 8), 2)
    )
    ones = jnp.ones((8, 128), F32)

    def mask_of(occ):
        spread = jnp.broadcast_to(occ[:, None, :], (8, 8, 8))
        picked = jnp.where(eye & (spread > 0), 1.0, 0.0).astype(F32).reshape(64, 8)
        return jnp.dot(picked, ones, preferred_element_type=F32)

    def mask_plane(i, carry):
        b, p = i // 8, lax.rem(i, 8)
        m = mask_of(occv[b, p])
        mask[i] = m
        keep = m > 0.5
        xk = jnp.where(keep, xv[b, p].astype(F32), 0.0)
        gk = jnp.where(keep, gv[b, p].astype(F32), 0.0)
        xm[i] = xk.reshape(8, 8, 128)
        gm[i] = gk.reshape(8, 8, 128)
        gmb[i] = gk.astype(BF)
        return carry

    lax.fori_loop(0, 16, mask_plane, 0, unroll=4)

    zi = lax.broadcasted_iota(jnp.int32, (10, 8, 128), 1)

    def weights_of(b, dx, local):
        wanted = (me_s + dx) * 2 + local

        def one(dy, dz):
            link = links[b, slot_of(dx, dy, dz)]
            return jnp.where((link == wanted) & (link >= 0), 1.0, 0.0).astype(F32)

        return one

    def put_plane(dst, index, centre, low, high):
        shifted = (
            pltpu.roll(jnp.where(zi == 7, low, centre), 1, 1),
            centre,
            pltpu.roll(jnp.where(zi == 0, high, centre), 7, 1),
        )
        for ty in range(3):
            for tz in range(3):
                col = (3 * ty + tz) * 128
                dst[index, :, col : col + 128] = (
                    shifted[tz][ty : ty + 8].reshape(64, 128).astype(BF)
                )

    def own_planes(src, dst):
        for b in range(2):
            one = weights_of(b, 0, 1 - b)
            w = {
                (dy, dz): one(dy, dz)
                for dy in (-1, 0, 1)
                for dz in (-1, 0, 1)
                if (dy, dz) != (0, 0)
            }

            def plane(p, carry, b=b, w=w):
                mine = src[8 * b + p]
                theirs = src[8 * (1 - b) + p]
                first, last = theirs[0:1], theirs[7:8]

                def zone(dz):
                    middle = mine if dz == 0 else theirs * w[0, dz]
                    return jnp.concatenate(
                        [last * w[-1, dz], middle, first * w[1, dz]], axis=0
                    )

                put_plane(dst, 10 * b + p + 1, zone(0), zone(-1), zone(1))
                return carry

            lax.fori_loop(0, 8, plane, 0)

    def rim_planes(halo, dst):
        for side, dx in ((0, -1), (1, 1)):
            p0, p1 = (
                jnp.where(
                    mask_of(halo_o[side, b]) > 0.5, halo[side, b].astype(F32), 0.0
                ).reshape(8, 8, 128)
                for b in range(2)
            )
            for b in range(2):
                w0 = weights_of(b, dx, 0)
                w1 = weights_of(b, dx, 1)

                def zone(dz):
                    def mix(dy, rows):
                        return p0[rows] * w0(dy, dz) + p1[rows] * w1(dy, dz)

                    return jnp.concatenate(
                        [mix(-1, slice(7, 8)), mix(0, slice(0, 8)), mix(1, slice(0, 1))],
                        axis=0,
                    )

                put_plane(dst, 10 * b + 9 * side, zone(0), zone(-1), zone(1))

    def kernel_grad(tx):
        for ty in range(3):
            total = None
            for b in range(2):
                window = xs[10 * b + tx : 10 * b + tx + 8, :, 384 * ty : 384 * ty + 384]
                part = jnp.dot(
                    gt[:, 512 * b : 512 * b + 512],
                    window.reshape(512, 384),
                    preferred_element_type=F32,
                )
                total = part if total is None else total + part
            for tz in range(3):
                tap = 9 * tx + 3 * ty + tz
                cbuf[128 * tap : 128 * tap + 128, :] = total[:, 128 * tz : 128 * tz + 128].T

    def core_copy(n):
        z0, nz = CHUNKS[n]
        return pltpu.make_async_remote_copy(
            src_ref=csnd.at[pl.ds(4 * z0, 4 * nz)],
            dst_ref=crcv.at[pl.ds(4 * z0, 4 * nz)],
            send_sem=core_s.at[n],
            recv_sem=core_r.at[n],
            device_id=partner,
            device_id_type=MESH,
        )

    def core_send(n):
        z0, nz = CHUNKS[n]

        def fill(j, carry):
            for q in range(4):
                csnd[j, q] = cbuf[pl.ds(ROWS * (2 * j + other_c) + PART * q, SLOT), :]
            return carry

        lax.fori_loop(4 * z0, 4 * (z0 + nz), fill, 0)
        core_copy(n).start()

    def xy_copy(n, k):
        z0, nz = CHUNKS[n]
        px, py = xy_peer(k)
        return pltpu.make_async_remote_copy(
            src_ref=xyb.at[px, py, pl.ds(z0, nz)],
            dst_ref=rxy.at[k - 1, pl.ds(z0, nz)],
            send_sem=xy_s.at[n, k - 1],
            recv_sem=xy_r.at[n, k - 1],
            device_id=at(py, me_z, px, me_c),
            device_id_type=MESH,
        )

    def xy_send(n):
        z0, nz = CHUNKS[n]
        core_copy(n).wait()

        def fill(j, carry):
            for q in range(4):
                mine = cbuf[pl.ds(ROWS * (2 * j + me_c) + PART * q, SLOT), :]
                xyb[lax.rem(j, 4), q, j // 4] = mine + crcv[j, q]
            return carry

        lax.fori_loop(4 * z0, 4 * (z0 + nz), fill, 0)

        def go(k, carry):
            xy_copy(n, k).start()
            return carry

        lax.fori_loop(1, 16, go, 0)

        def keep(z, carry):
            j = 4 * z + me_x
            own[z] = (
                cbuf[pl.ds(ROWS * (2 * j + me_c) + PART * me_y, SLOT), :]
                + crcv[j, me_y]
            )
            return carry

        lax.fori_loop(z0, z0 + nz, keep, 0)

    def z_copy(slot, target):
        return pltpu.make_async_remote_copy(
            src_ref=zp.at[target],
            dst_ref=rz.at[slot],
            send_sem=z_s.at[target],
            recv_sem=z_r.at[slot],
            device_id=at(me_y, target, me_x, me_c),
            device_id_type=MESH,
        )

    def z_send(n):
        z0, nz = CHUNKS[n]

        def arrived(k, carry):
            xy_copy(n, k).wait()
            return carry

        lax.fori_loop(1, 16, arrived, 0)

        def add(z, carry):
            total = own[z]
            for k in range(15):
                total = total + rxy[k, z]
            zp[z] = total

            @pl.when(z != me_z)
            def _():
                z_copy(me_z, z).start()

            return carry

        lax.fori_loop(z0, z0 + nz, add, 0)

    def transposed_weights():
        def turn(t, carry):
            wt[26 - t] = wv[t].T
            return carry

        lax.fori_loop(0, 27, turn, 0)

    def product(shifts, taps, out_index, out_hbm, part):
        b = part // 2
        start = 10 * b + 4 * lax.rem(part, 2)
        total = None
        for tx in range(3):
            window = shifts[pl.ds(start + tx, 4)].reshape(256, 1152)
            piece = jnp.dot(
                window, taps[9 * tx : 9 * tx + 9].reshape(1152, 128),
                preferred_element_type=F32,
            )
            total = piece if total is None else total + piece
        planes = pl.ds(4 * part, 4)
        keep = mask[planes].reshape(256, 128) > 0.5
        outv[out_index, planes] = jnp.where(keep, total, 0.0).astype(BF).reshape(4, 64, 128)

    def products(shifts, taps, out_index, out_hbm, lo, hi):
        def one(part, carry):
            product(shifts, taps, out_index, out_hbm, part)
            return carry

        lax.fori_loop(lo, hi, one, 0)

    def out_copy(index):
        dst = (resp_hbm, gin_hbm)[index]
        return pltpu.make_async_copy(outv.at[index], dst, out_sem.at[index])

    cbuf[128 * 27 :, :] = jnp.zeros((SLOT, 128), F32)
    own_planes(xm, xs)
    for k in range(8):
        gt[:, 128 * k : 128 * k + 128] = gmb[2 * k : 2 * k + 2].reshape(128, 128).T
    kernel_grad(1)
    core_send(0)
    round_wait(0)
    round_signal(1)
    for side in range(2):
        halos[side][0].wait()
        halos[side][1].wait()
    rim_planes(halo_x, xs)
    kernel_grad(0)
    core_send(1)
    round_wait(1)
    round_signal(2)
    kernel_grad(2)
    core_send(2)
    round_wait(2)
    xy_send(0)
    xy_send(1)
    own_planes(gm, gs)
    xy_send(2)

    loads[3].wait()
    z_send(0)
    products(xs, wv, 0, resp_hbm, 0, 2)
    z_send(1)
    products(xs, wv, 0, resp_hbm, 2, 4)
    out_copy(0).start()
    z_send(2)
    halos[0][2].wait()
    halos[1][2].wait()
    rim_planes(halo_g, gs)
    transposed_weights()
    products(gs, wt, 1, gin_hbm, 0, 2)

    def z_done(k, carry):
        source = lax.rem(me_z + k, 8)
        z_copy(source, source).wait_recv()
        z_copy(me_z, source).wait_send()
        return carry

    lax.fori_loop(1, 8, z_done, 0)
    rz[me_z] = zp[me_z]
    total = rz[0]
    for z in range(1, 8):
        total = total + rz[z]
    fin[me_y] = total * (1.0 / math.sqrt(4 * 128 * 8**3))

    def y_copy(slot, k):
        return pltpu.make_async_remote_copy(
            src_ref=fin.at[me_y],
            dst_ref=fin.at[slot],
            send_sem=y_s.at[k],
            recv_sem=y_r.at[slot],
            device_id=at(lax.rem(me_y + k, 4), me_z, me_x, me_c),
            device_id_type=MESH,
        )

    for k in range(1, 4):
        y_copy(me_y, k).start()
    products(gs, wt, 1, gin_hbm, 2, 4)
    out_copy(1).start()
    for k in range(1, 4):
        y_copy(lax.rem(me_y + k, 4), k).wait_recv()
        y_copy(me_y, k).wait_send()
    for q in range(4):
        rows = min(PART, ROWS - PART * q)
        gw_ref[PART * q : PART * q + rows, :] = fin[q, :rows]
    out_copy(0).wait()
    out_copy(1).wait()


def per_device(features, occupancy, neighbours, weight, cotangent):
    dma = pltpu.SemaphoreType.DMA
    anywhere = pl.BlockSpec(memory_space=pl.ANY)
    resp, gin, gw = pl.pallas_call(
        kernel,
        out_shape=(
            jax.ShapeDtypeStruct((16, 64, 128), BF),
            jax.ShapeDtypeStruct((16, 64, 128), BF),
            jax.ShapeDtypeStruct((ROWS, 128), F32),
        ),
        in_specs=[
            anywhere,
            anywhere,
            anywhere,
            pl.BlockSpec(memory_space=pltpu.SMEM),
            anywhere,
        ],
        out_specs=(anywhere, anywhere, pl.BlockSpec(memory_space=pltpu.VMEM)),
        scratch_shapes=[
            pltpu.VMEM((2, 8, 64, 128), BF),
            pltpu.VMEM((2, 8, 64, 128), BF),
            pltpu.VMEM((2, 8, 8, 8), jnp.int32),
            pltpu.VMEM((27, 128, 128), BF),
            pltpu.VMEM((27, 128, 128), BF),
            pltpu.VMEM((16, 64, 128), F32),
            pltpu.VMEM((16, 8, 8, 128), F32),
            pltpu.VMEM((16, 8, 8, 128), F32),
            pltpu.VMEM((16, 64, 128), BF),
            pltpu.VMEM((128, 1024), BF),
            pltpu.VMEM((20, 64, 1152), BF),
            pltpu.VMEM((20, 64, 1152), BF),
            pltpu.VMEM((2, 2, 64, 128), BF),
            pltpu.VMEM((2, 2, 64, 128), BF),
            pltpu.VMEM((2, 2, 8, 8), jnp.int32),
            pltpu.VMEM((3472, 128), F32),
            pltpu.VMEM((32, 4, SLOT, 128), F32),
            pltpu.VMEM((32, 4, SLOT, 128), F32),
            pltpu.VMEM((4, 4, 8, SLOT, 128), F32),
            pltpu.VMEM((8, SLOT, 128), F32),
            pltpu.VMEM((15, 8, SLOT, 128), F32),
            pltpu.VMEM((8, SLOT, 128), F32),
            pltpu.VMEM((8, SLOT, 128), F32),
            pltpu.VMEM((4, SLOT, 128), F32),
            pltpu.VMEM((2, 16, 64, 128), BF),
            dma((4,)),
            dma((2,)),
            dma((3, 2)),
            dma((3, 2)),
            dma((3,)),
            dma((3,)),
            dma((3, 15)),
            dma((3, 15)),
            dma((8,)),
            dma((8,)),
            dma((4,)),
            dma((4,)),
            pltpu.SemaphoreType.REGULAR((3,)),
        ],
        compiler_params=pltpu.CompilerParams(collective_id=0, has_side_effects=True),
        name="sparse_conv_step",
    )(
        features.reshape(2, 8, 64, 128),
        cotangent.reshape(2, 8, 64, 128),
        occupancy[0],
        neighbours[0],
        weight,
    )
    shape = features.shape
    return resp.reshape(shape), gin.reshape(shape), gw


def solution(mesh):
    placed = (
        P("dp", "space", None, None, None, None),
        P("dp", "space", None, None, None),
        P("dp", "space", None),
        P(),
        P("dp", "space", None, None, None, None),
    )
    return jax.shard_map(
        per_device,
        mesh=mesh,
        in_specs=placed,
        out_specs=(
            P("dp", "space", None, None, None, None),
            P("dp", "space", None, None, None, None),
            P("space", None),
        ),
        check_vma=False,
    )
```

```python
import functools
import math

import jax
import jax.numpy as jnp
from jax import lax
from jax.experimental import pallas as pl
from jax.experimental.pallas import tpu as pltpu
from jax.sharding import PartitionSpec as P

MESH = pl.DeviceIdType.MESH
BF = jnp.bfloat16
F32 = jnp.float32
ROWS = 54
PART = 14
SLOT = 16
CHUNKS = ((3, 2), (0, 3), (5, 3))


def slot_of(dx, dy, dz):
    number = 9 * (dx + 1) + 3 * (dy + 1) + (dz + 1)
    return number if number < 13 else number - 1


def kernel(
    x_hbm, g_hbm, occ_hbm, links, w_hbm,
    resp_hbm, gin_hbm, gw_ref,
    xv, gv, occv, wv, wt, mask, xm, gm, gmb, gt, xs, gs,
    halo_x, halo_g, halo_o, cbuf, csnd, crcv, xyb, own, rxy, zp, rz, fin, outv,
    in_sem, out_sem, halo_s, halo_r, core_s, core_r, xy_s, xy_r, z_s, z_r, y_s, y_r, ready,
):
    me_y = lax.axis_index("dp")
    me_s = lax.axis_index("space")
    me_c = lax.rem(me_s, 2)
    me_x = lax.rem(me_s // 2, 4)
    me_z = me_s // 8
    other_c = 1 - me_c

    def at(y, z, x, c):
        return (y, (z * 4 + x) * 2 + c)

    after = (me_y, lax.rem(me_s + 1, 64))
    before = (me_y, lax.rem(me_s + 63, 64))
    partner = at(me_y, me_z, me_x, other_c)

    def xy_peer(k):
        return lax.rem(me_x + k // 4, 4), lax.rem(me_y + lax.rem(k, 4), 4)

    loads = [
        pltpu.make_async_copy(src, dst, in_sem.at[i])
        for i, (src, dst) in enumerate(
            ((occ_hbm, occv), (x_hbm, xv), (g_hbm, gv), (w_hbm, wv))
        )
    ]
    for load in loads:
        load.start()

    barrier = pltpu.get_barrier_semaphore()

    def greet(device):
        pl.semaphore_signal(barrier, inc=1, device_id=device, device_id_type=MESH)

    near = [
        at(me_y, me_z, lax.rem(me_x + d, 4), me_c) for d in (1, 3)
    ] + [
        at(lax.rem(me_y + d, 4), me_z, me_x, me_c) for d in (1, 3)
    ] + [
        at(me_y, lax.rem(me_z + d, 8), me_x, me_c) for d in (1, 7)
    ]
    for device in [before, after, partner] + near:
        greet(device)

    def round_signal(r):
        for device in near:
            pl.semaphore_signal(ready.at[r], inc=1, device_id=device, device_id_type=MESH)

    def round_wait(r):
        pl.semaphore_wait(ready.at[r], 6)

    pl.semaphore_wait(barrier, 9)

    def halo_copies(side):
        plane = 7 * side
        return [
            pltpu.make_async_remote_copy(
                src_ref=src.at[:, plane],
                dst_ref=dst.at[1 - side],
                send_sem=halo_s.at[t, side],
                recv_sem=halo_r.at[t, 1 - side],
                device_id=after if side == 1 else before,
                device_id_type=MESH,
            )
            for t, (src, dst) in enumerate(
                ((occ_hbm, halo_o), (x_hbm, halo_x), (g_hbm, halo_g))
            )
        ]

    halos = [halo_copies(0), halo_copies(1)]
    for t in range(3):
        for side in range(2):
            halos[side][t].start()
    round_signal(0)

    for load in loads[:3]:
        load.wait()

    eye = (
        lax.broadcasted_iota(jnp.int32, (8, 8, 8), 1)
        == lax.broadcasted_iota(jnp.int32, (8, 8, 8), 2)
    )
    ones = jnp.ones((8, 128), F32)

    def mask_of(occ):
        spread = jnp.broadcast_to(occ[:, None, :], (8, 8, 8))
        picked = jnp.where(eye & (spread > 0), 1.0, 0.0).astype(F32).reshape(64, 8)
        return jnp.dot(picked, ones, preferred_element_type=F32)

    def mask_plane(i, carry):
        b, p = i // 8, lax.rem(i, 8)
        m = mask_of(occv[b, p])
        mask[i] = m
        keep = m > 0.5
        xk = jnp.where(keep, xv[b, p].astype(F32), 0.0)
        gk = jnp.where(keep, gv[b, p].astype(F32), 0.0)
        xm[i] = xk.reshape(8, 8, 128)
        gm[i] = gk.reshape(8, 8, 128)
        gmb[i] = gk.astype(BF)
        return carry

    lax.fori_loop(0, 16, mask_plane, 0, unroll=4)

    zi = lax.broadcasted_iota(jnp.int32, (10, 8, 128), 1)

    def weights_of(b, dx, local):
        wanted = (me_s + dx) * 2 + local

        def one(dy, dz):
            link = links[b, slot_of(dx, dy, dz)]
            return jnp.where((link == wanted) & (link >= 0), 1.0, 0.0).astype(F32)

        return one

    def put_plane(dst, index, centre, low, high):
        shifted = (
            pltpu.roll(jnp.where(zi == 7, low, centre), 1, 1),
            centre,
            pltpu.roll(jnp.where(zi == 0, high, centre), 7, 1),
        )
        for ty in range(3):
            for tz in range(3):
                col = (3 * ty + tz) * 128
                dst[index, :, col : col + 128] = (
                    shifted[tz][ty : ty + 8].reshape(64, 128).astype(BF)
                )

    def own_planes(src, dst):
        for b in range(2):
            one = weights_of(b, 0, 1 - b)
            w = {
                (dy, dz): one(dy, dz)
                for dy in (-1, 0, 1)
                for dz in (-1, 0, 1)
                if (dy, dz) != (0, 0)
            }

            def plane(p, carry, b=b, w=w):
                mine = src[8 * b + p]
                theirs = src[8 * (1 - b) + p]
                first, last = theirs[0:1], theirs[7:8]

                def zone(dz):
                    middle = mine if dz == 0 else theirs * w[0, dz]
                    return jnp.concatenate(
                        [last * w[-1, dz], middle, first * w[1, dz]], axis=0
                    )

                put_plane(dst, 10 * b + p + 1, zone(0), zone(-1), zone(1))
                return carry

            lax.fori_loop(0, 8, plane, 0)

    def rim_planes(halo, dst):
        for side, dx in ((0, -1), (1, 1)):
            p0, p1 = (
                jnp.where(
                    mask_of(halo_o[side, b]) > 0.5, halo[side, b].astype(F32), 0.0
                ).reshape(8, 8, 128)
                for b in range(2)
            )
            for b in range(2):
                w0 = weights_of(b, dx, 0)
                w1 = weights_of(b, dx, 1)

                def zone(dz):
                    def mix(dy, rows):
                        return p0[rows] * w0(dy, dz) + p1[rows] * w1(dy, dz)

                    return jnp.concatenate(
                        [mix(-1, slice(7, 8)), mix(0, slice(0, 8)), mix(1, slice(0, 1))],
                        axis=0,
                    )

                put_plane(dst, 10 * b + 9 * side, zone(0), zone(-1), zone(1))

    def kernel_grad(tx):
        for ty in range(3):
            total = None
            for b in range(2):
                window = xs[10 * b + tx : 10 * b + tx + 8, :, 384 * ty : 384 * ty + 384]
                part = jnp.dot(
                    gt[:, 512 * b : 512 * b + 512],
                    window.reshape(512, 384),
                    preferred_element_type=F32,
                )
                total = part if total is None else total + part
            for tz in range(3):
                tap = 9 * tx + 3 * ty + tz
                cbuf[128 * tap : 128 * tap + 128, :] = total[:, 128 * tz : 128 * tz + 128].T

    def core_copy(n):
        z0, nz = CHUNKS[n]
        return pltpu.make_async_remote_copy(
            src_ref=csnd.at[pl.ds(4 * z0, 4 * nz)],
            dst_ref=crcv.at[pl.ds(4 * z0, 4 * nz)],
            send_sem=core_s.at[n],
            recv_sem=core_r.at[n],
            device_id=partner,
            device_id_type=MESH,
        )

    def core_send(n):
        z0, nz = CHUNKS[n]

        def fill(j, carry):
            for q in range(4):
                csnd[j, q] = cbuf[pl.ds(ROWS * (2 * j + other_c) + PART * q, SLOT), :]
            return carry

        lax.fori_loop(4 * z0, 4 * (z0 + nz), fill, 0)
        core_copy(n).start()

    row_of = lax.broadcasted_iota(jnp.int32, (SLOT, 128), 0)

    def coded(v):
        top = jnp.max(jnp.abs(v), axis=0, keepdims=True)
        power = jnp.ceil(jnp.log2(jnp.maximum(top, 2e-33) * (1.0 / 32000.0)))
        return (
            jnp.where(row_of == PART, power, jnp.round(v * jnp.exp2(-power)))
            .astype(jnp.int32)
            .astype(jnp.int16)
        )

    def decoded(c):
        v = c.astype(jnp.int32).astype(F32)
        return v * jnp.exp2(v[PART : PART + 1])

    def xy_copy(n, k):
        z0, nz = CHUNKS[n]
        px, py = xy_peer(k)
        return pltpu.make_async_remote_copy(
            src_ref=xyb.at[px, py, pl.ds(z0, nz)],
            dst_ref=rxy.at[k - 1, pl.ds(z0, nz)],
            send_sem=xy_s.at[n, k - 1],
            recv_sem=xy_r.at[n, k - 1],
            device_id=at(py, me_z, px, me_c),
            device_id_type=MESH,
        )

    def xy_send(n):
        z0, nz = CHUNKS[n]
        core_copy(n).wait()

        def fill(j, carry):
            for q in range(4):
                mine = cbuf[pl.ds(ROWS * (2 * j + me_c) + PART * q, SLOT), :]
                xyb[lax.rem(j, 4), q, j // 4] = coded(mine + crcv[j, q])
            return carry

        lax.fori_loop(4 * z0, 4 * (z0 + nz), fill, 0)

        def go(k, carry):
            xy_copy(n, k).start()
            return carry

        lax.fori_loop(1, 16, go, 0)

        def keep(z, carry):
            j = 4 * z + me_x
            own[z] = (
                cbuf[pl.ds(ROWS * (2 * j + me_c) + PART * me_y, SLOT), :]
                + crcv[j, me_y]
            )
            return carry

        lax.fori_loop(z0, z0 + nz, keep, 0)

    def z_copy(slot, target):
        return pltpu.make_async_remote_copy(
            src_ref=zp.at[target],
            dst_ref=rz.at[slot],
            send_sem=z_s.at[target],
            recv_sem=z_r.at[slot],
            device_id=at(me_y, target, me_x, me_c),
            device_id_type=MESH,
        )

    def z_send(n):
        z0, nz = CHUNKS[n]

        def arrived(k, carry):
            xy_copy(n, k).wait()
            return carry

        lax.fori_loop(1, 16, arrived, 0)

        def add(z, carry):
            total = own[z]
            for k in range(15):
                total = total + decoded(rxy[k, z])
            zp[z] = total

            @pl.when(z != me_z)
            def _():
                z_copy(me_z, z).start()

            return carry

        lax.fori_loop(z0, z0 + nz, add, 0)

    def transposed_weights():
        def turn(t, carry):
            wt[26 - t] = wv[t].T
            return carry

        lax.fori_loop(0, 27, turn, 0)

    def product(shifts, taps, out_index, out_hbm, part):
        b = part // 2
        start = 10 * b + 4 * lax.rem(part, 2)
        total = None
        for tx in range(3):
            window = shifts[pl.ds(start + tx, 4)].reshape(256, 1152)
            piece = jnp.dot(
                window, taps[9 * tx : 9 * tx + 9].reshape(1152, 128),
                preferred_element_type=F32,
            )
            total = piece if total is None else total + piece
        planes = pl.ds(4 * part, 4)
        keep = mask[planes].reshape(256, 128) > 0.5
        outv[out_index, planes] = jnp.where(keep, total, 0.0).astype(BF).reshape(4, 64, 128)

    def products(shifts, taps, out_index, out_hbm, lo, hi):
        def one(part, carry):
            product(shifts, taps, out_index, out_hbm, part)
            return carry

        lax.fori_loop(lo, hi, one, 0)

    def out_copy(index):
        dst = (resp_hbm, gin_hbm)[index]
        return pltpu.make_async_copy(outv.at[index], dst, out_sem.at[index])

    cbuf[128 * 27 :, :] = jnp.zeros((SLOT, 128), F32)
    own_planes(xm, xs)
    for k in range(8):
        gt[:, 128 * k : 128 * k + 128] = gmb[2 * k : 2 * k + 2].reshape(128, 128).T
    kernel_grad(1)
    core_send(0)
    round_wait(0)
    round_signal(1)
    for side in range(2):
        halos[side][0].wait()
        halos[side][1].wait()
    rim_planes(halo_x, xs)
    kernel_grad(0)
    core_send(1)
    round_wait(1)
    round_signal(2)
    kernel_grad(2)
    core_send(2)
    round_wait(2)
    xy_send(0)
    xy_send(1)
    loads[3].wait()
    products(xs, wv, 0, resp_hbm, 0, 1)
    xy_send(2)
    own_planes(gm, gs)
    halos[0][2].wait()
    halos[1][2].wait()
    rim_planes(halo_g, gs)
    transposed_weights()
    products(xs, wv, 0, resp_hbm, 1, 4)
    out_copy(0).start()
    z_send(0)
    z_send(1)
    z_send(2)
    products(gs, wt, 1, gin_hbm, 0, 3)

    def z_done(k, carry):
        source = lax.rem(me_z + k, 8)
        z_copy(source, source).wait_recv()
        z_copy(me_z, source).wait_send()
        return carry

    lax.fori_loop(1, 8, z_done, 0)
    rz[me_z] = zp[me_z]
    total = rz[0]
    for z in range(1, 8):
        total = total + rz[z]
    fin[me_y] = total * (1.0 / math.sqrt(4 * 128 * 8**3))

    def y_copy(slot, k):
        return pltpu.make_async_remote_copy(
            src_ref=fin.at[me_y],
            dst_ref=fin.at[slot],
            send_sem=y_s.at[k],
            recv_sem=y_r.at[slot],
            device_id=at(lax.rem(me_y + k, 4), me_z, me_x, me_c),
            device_id_type=MESH,
        )

    for k in range(1, 4):
        y_copy(me_y, k).start()
    products(gs, wt, 1, gin_hbm, 3, 4)
    out_copy(1).start()
    for k in range(1, 4):
        y_copy(lax.rem(me_y + k, 4), k).wait_recv()
        y_copy(me_y, k).wait_send()
    for q in range(4):
        rows = min(PART, ROWS - PART * q)
        gw_ref[PART * q : PART * q + rows, :] = fin[q, :rows]
    out_copy(0).wait()
    out_copy(1).wait()


def per_device(features, occupancy, neighbours, weight, cotangent):
    dma = pltpu.SemaphoreType.DMA
    anywhere = pl.BlockSpec(memory_space=pl.ANY)
    resp, gin, gw = pl.pallas_call(
        kernel,
        out_shape=(
            jax.ShapeDtypeStruct((16, 64, 128), BF),
            jax.ShapeDtypeStruct((16, 64, 128), BF),
            jax.ShapeDtypeStruct((ROWS, 128), F32),
        ),
        in_specs=[
            anywhere,
            anywhere,
            anywhere,
            pl.BlockSpec(memory_space=pltpu.SMEM),
            anywhere,
        ],
        out_specs=(anywhere, anywhere, pl.BlockSpec(memory_space=pltpu.VMEM)),
        scratch_shapes=[
            pltpu.VMEM((2, 8, 64, 128), BF),
            pltpu.VMEM((2, 8, 64, 128), BF),
            pltpu.VMEM((2, 8, 8, 8), jnp.int32),
            pltpu.VMEM((27, 128, 128), BF),
            pltpu.VMEM((27, 128, 128), BF),
            pltpu.VMEM((16, 64, 128), F32),
            pltpu.VMEM((16, 8, 8, 128), F32),
            pltpu.VMEM((16, 8, 8, 128), F32),
            pltpu.VMEM((16, 64, 128), BF),
            pltpu.VMEM((128, 1024), BF),
            pltpu.VMEM((20, 64, 1152), BF),
            pltpu.VMEM((20, 64, 1152), BF),
            pltpu.VMEM((2, 2, 64, 128), BF),
            pltpu.VMEM((2, 2, 64, 128), BF),
            pltpu.VMEM((2, 2, 8, 8), jnp.int32),
            pltpu.VMEM((3472, 128), F32),
            pltpu.VMEM((32, 4, SLOT, 128), F32),
            pltpu.VMEM((32, 4, SLOT, 128), F32),
            pltpu.VMEM((4, 4, 8, SLOT, 128), jnp.int16),
            pltpu.VMEM((8, SLOT, 128), F32),
            pltpu.VMEM((15, 8, SLOT, 128), jnp.int16),
            pltpu.VMEM((8, SLOT, 128), F32),
            pltpu.VMEM((8, SLOT, 128), F32),
            pltpu.VMEM((4, SLOT, 128), F32),
            pltpu.VMEM((2, 16, 64, 128), BF),
            dma((4,)),
            dma((2,)),
            dma((3, 2)),
            dma((3, 2)),
            dma((3,)),
            dma((3,)),
            dma((3, 15)),
            dma((3, 15)),
            dma((8,)),
            dma((8,)),
            dma((4,)),
            dma((4,)),
            pltpu.SemaphoreType.REGULAR((3,)),
        ],
        compiler_params=pltpu.CompilerParams(collective_id=0, has_side_effects=True),
        name="sparse_conv_step",
    )(
        features.reshape(2, 8, 64, 128),
        cotangent.reshape(2, 8, 64, 128),
        occupancy[0],
        neighbours[0],
        weight,
    )
    shape = features.shape
    return resp.reshape(shape), gin.reshape(shape), gw


def solution(mesh):
    placed = (
        P("dp", "space", None, None, None, None),
        P("dp", "space", None, None, None),
        P("dp", "space", None),
        P(),
        P("dp", "space", None, None, None, None),
    )
    return jax.shard_map(
        per_device,
        mesh=mesh,
        in_specs=placed,
        out_specs=(
            P("dp", "space", None, None, None, None),
            P("dp", "space", None, None, None, None),
            P("space", None),
        ),
        check_vma=False,
    )
```

```python
import functools
import math

import jax
import jax.numpy as jnp
from jax import lax
from jax.experimental import pallas as pl
from jax.experimental.pallas import tpu as pltpu
from jax.sharding import PartitionSpec as P

MESH = pl.DeviceIdType.MESH
BF = jnp.bfloat16
F32 = jnp.float32
ROWS = 54
PART = 14
SLOT = 16
CHUNKS = ((3, 2), (0, 3), (5, 3))


def slot_of(dx, dy, dz):
    number = 9 * (dx + 1) + 3 * (dy + 1) + (dz + 1)
    return number if number < 13 else number - 1


def kernel(
    x_hbm, g_hbm, occ_hbm, links, w_hbm,
    resp_ref, gin_ref, gw_ref,
    xv, gv, occv, wv, wt, mask, xm, gm, gmb, gt, xs, gs,
    halo_x, halo_g, halo_o, cbuf, csnd, crcv, xyb, own, rxy, zp, rz, fin,
    in_sem, halo_s, halo_r, core_s, core_r, xy_s, xy_r, z_s, z_r, y_s, y_r, ready,
):
    me_y = lax.axis_index("dp")
    me_s = lax.axis_index("space")
    me_c = lax.rem(me_s, 2)
    me_x = lax.rem(me_s // 2, 4)
    me_z = me_s // 8
    other_c = 1 - me_c

    def at(y, z, x, c):
        return (y, (z * 4 + x) * 2 + c)

    after = (me_y, lax.rem(me_s + 1, 64))
    before = (me_y, lax.rem(me_s + 63, 64))
    partner = at(me_y, me_z, me_x, other_c)

    def xy_peer(k):
        return lax.rem(me_x + k // 4, 4), lax.rem(me_y + lax.rem(k, 4), 4)

    loads = [
        pltpu.make_async_copy(src, dst, in_sem.at[i])
        for i, (src, dst) in enumerate(
            ((occ_hbm, occv), (x_hbm, xv), (g_hbm, gv), (w_hbm, wv))
        )
    ]
    for load in loads:
        load.start()

    barrier = pltpu.get_barrier_semaphore()

    def greet(device):
        pl.semaphore_signal(barrier, inc=1, device_id=device, device_id_type=MESH)

    near = [
        at(me_y, me_z, lax.rem(me_x + d, 4), me_c) for d in (1, 3)
    ] + [
        at(lax.rem(me_y + d, 4), me_z, me_x, me_c) for d in (1, 3)
    ] + [
        at(me_y, lax.rem(me_z + d, 8), me_x, me_c) for d in (1, 7)
    ]
    for device in [before, after, partner] + near:
        greet(device)

    def round_signal(r):
        for device in near:
            pl.semaphore_signal(ready.at[r], inc=1, device_id=device, device_id_type=MESH)

    def round_wait(r):
        pl.semaphore_wait(ready.at[r], 6)

    pl.semaphore_wait(barrier, 9)

    def halo_copies(side):
        plane = 7 * side
        return [
            pltpu.make_async_remote_copy(
                src_ref=src.at[:, plane],
                dst_ref=dst.at[1 - side],
                send_sem=halo_s.at[t, side],
                recv_sem=halo_r.at[t, 1 - side],
                device_id=after if side == 1 else before,
                device_id_type=MESH,
            )
            for t, (src, dst) in enumerate(
                ((occ_hbm, halo_o), (x_hbm, halo_x), (g_hbm, halo_g))
            )
        ]

    halos = [halo_copies(0), halo_copies(1)]
    for t in range(3):
        for side in range(2):
            halos[side][t].start()
    round_signal(0)

    for load in loads[:3]:
        load.wait()

    eye = (
        lax.broadcasted_iota(jnp.int32, (8, 8, 8), 1)
        == lax.broadcasted_iota(jnp.int32, (8, 8, 8), 2)
    )
    ones = jnp.ones((8, 128), F32)

    def mask_of(occ):
        spread = jnp.broadcast_to(occ[:, None, :], (8, 8, 8))
        picked = jnp.where(eye & (spread > 0), 1.0, 0.0).astype(F32).reshape(64, 8)
        return jnp.dot(picked, ones, preferred_element_type=F32)

    def mask_plane(i, carry):
        b, p = i // 8, lax.rem(i, 8)
        m = mask_of(occv[b, p])
        mask[i] = m
        keep = m > 0.5
        xk = jnp.where(keep, xv[b, p].astype(F32), 0.0)
        gk = jnp.where(keep, gv[b, p].astype(F32), 0.0)
        xm[i] = xk.reshape(8, 8, 128)
        gm[i] = gk.reshape(8, 8, 128)
        gmb[i] = gk.astype(BF)
        return carry

    lax.fori_loop(0, 16, mask_plane, 0, unroll=4)

    zi = lax.broadcasted_iota(jnp.int32, (10, 8, 128), 1)

    def weights_of(b, dx, local):
        wanted = (me_s + dx) * 2 + local

        def one(dy, dz):
            link = links[b, slot_of(dx, dy, dz)]
            return jnp.where((link == wanted) & (link >= 0), 1.0, 0.0).astype(F32)

        return one

    def put_plane(dst, index, centre, low, high):
        shifted = (
            pltpu.roll(jnp.where(zi == 7, low, centre), 1, 1),
            centre,
            pltpu.roll(jnp.where(zi == 0, high, centre), 7, 1),
        )
        for ty in range(3):
            for tz in range(3):
                col = (3 * ty + tz) * 128
                dst[index, :, col : col + 128] = (
                    shifted[tz][ty : ty + 8].reshape(64, 128).astype(BF)
                )

    def own_planes(src, dst):
        for b in range(2):
            one = weights_of(b, 0, 1 - b)
            w = {
                (dy, dz): one(dy, dz)
                for dy in (-1, 0, 1)
                for dz in (-1, 0, 1)
                if (dy, dz) != (0, 0)
            }

            def plane(p, carry, b=b, w=w):
                mine = src[8 * b + p]
                theirs = src[8 * (1 - b) + p]
                first, last = theirs[0:1], theirs[7:8]

                def zone(dz):
                    middle = mine if dz == 0 else theirs * w[0, dz]
                    return jnp.concatenate(
                        [last * w[-1, dz], middle, first * w[1, dz]], axis=0
                    )

                put_plane(dst, 10 * b + p + 1, zone(0), zone(-1), zone(1))
                return carry

            lax.fori_loop(0, 8, plane, 0)

    def rim_planes(halo, dst):
        for side, dx in ((0, -1), (1, 1)):
            p0, p1 = (
                jnp.where(
                    mask_of(halo_o[side, b]) > 0.5, halo[side, b].astype(F32), 0.0
                ).reshape(8, 8, 128)
                for b in range(2)
            )
            for b in range(2):
                w0 = weights_of(b, dx, 0)
                w1 = weights_of(b, dx, 1)

                def zone(dz):
                    def mix(dy, rows):
                        return p0[rows] * w0(dy, dz) + p1[rows] * w1(dy, dz)

                    return jnp.concatenate(
                        [mix(-1, slice(7, 8)), mix(0, slice(0, 8)), mix(1, slice(0, 1))],
                        axis=0,
                    )

                put_plane(dst, 10 * b + 9 * side, zone(0), zone(-1), zone(1))

    def kernel_grad(tx):
        for ty in range(3):
            total = None
            for b in range(2):
                window = xs[10 * b + tx : 10 * b + tx + 8, :, 384 * ty : 384 * ty + 384]
                part = jnp.dot(
                    gt[:, 512 * b : 512 * b + 512],
                    window.reshape(512, 384),
                    preferred_element_type=F32,
                )
                total = part if total is None else total + part
            for tz in range(3):
                tap = 9 * tx + 3 * ty + tz
                cbuf[128 * tap : 128 * tap + 128, :] = total[:, 128 * tz : 128 * tz + 128].T

    def core_copy(n):
        z0, nz = CHUNKS[n]
        return pltpu.make_async_remote_copy(
            src_ref=csnd.at[pl.ds(4 * z0, 4 * nz)],
            dst_ref=crcv.at[pl.ds(4 * z0, 4 * nz)],
            send_sem=core_s.at[n],
            recv_sem=core_r.at[n],
            device_id=partner,
            device_id_type=MESH,
        )

    def core_send(n):
        z0, nz = CHUNKS[n]

        def fill(j, carry):
            for q in range(4):
                csnd[j, q] = cbuf[pl.ds(ROWS * (2 * j + other_c) + PART * q, SLOT), :]
            return carry

        lax.fori_loop(4 * z0, 4 * (z0 + nz), fill, 0, unroll=4)
        core_copy(n).start()

    row_of = lax.broadcasted_iota(jnp.int32, (SLOT, 128), 0)

    def coded(v):
        top = jnp.max(jnp.abs(v), axis=0, keepdims=True)
        power = jnp.ceil(jnp.log2(jnp.maximum(top, 2e-33) * (1.0 / 32000.0)))
        return (
            jnp.where(row_of == PART, power, jnp.round(v * jnp.exp2(-power)))
            .astype(jnp.int32)
            .astype(jnp.int16)
        )

    def decoded(c):
        v = c.astype(jnp.int32).astype(F32)
        return v * jnp.exp2(v[PART : PART + 1])

    def xy_copy(n, k):
        z0, nz = CHUNKS[n]
        px, py = xy_peer(k)
        return pltpu.make_async_remote_copy(
            src_ref=xyb.at[px, py, pl.ds(z0, nz)],
            dst_ref=rxy.at[k - 1, pl.ds(z0, nz)],
            send_sem=xy_s.at[n, k - 1],
            recv_sem=xy_r.at[n, k - 1],
            device_id=at(py, me_z, px, me_c),
            device_id_type=MESH,
        )

    def xy_send(n):
        z0, nz = CHUNKS[n]
        core_copy(n).wait()

        def fill(j, carry):
            for q in range(4):
                mine = cbuf[pl.ds(ROWS * (2 * j + me_c) + PART * q, SLOT), :]
                xyb[lax.rem(j, 4), q, j // 4] = coded(mine + crcv[j, q])
            return carry

        lax.fori_loop(4 * z0, 4 * (z0 + nz), fill, 0, unroll=4)

        def go(k, carry):
            xy_copy(n, k).start()
            return carry

        lax.fori_loop(1, 16, go, 0)

        def keep(z, carry):
            j = 4 * z + me_x
            own[z] = (
                cbuf[pl.ds(ROWS * (2 * j + me_c) + PART * me_y, SLOT), :]
                + crcv[j, me_y]
            )
            return carry

        lax.fori_loop(z0, z0 + nz, keep, 0)

    def z_copy(slot, target):
        return pltpu.make_async_remote_copy(
            src_ref=zp.at[target],
            dst_ref=rz.at[slot],
            send_sem=z_s.at[target],
            recv_sem=z_r.at[slot],
            device_id=at(me_y, target, me_x, me_c),
            device_id_type=MESH,
        )

    def z_send(n):
        z0, nz = CHUNKS[n]

        def arrived(k, carry):
            xy_copy(n, k).wait()
            return carry

        lax.fori_loop(1, 16, arrived, 0)

        def add(z, carry):
            total = own[z]
            for k in range(15):
                total = total + decoded(rxy[k, z])
            zp[z] = total
            return carry

        lax.fori_loop(z0, z0 + nz, add, 0, unroll=True)

        def send(z, carry):
            @pl.when(z != me_z)
            def _():
                z_copy(me_z, z).start()

            return carry

        lax.fori_loop(z0, z0 + nz, send, 0)

    def transposed_weights():
        def turn(t, carry):
            wt[26 - t] = wv[t].T
            return carry

        lax.fori_loop(0, 27, turn, 0)

    def product(shifts, taps, out, part):
        b = part // 2
        start = 10 * b + 4 * lax.rem(part, 2)
        total = None
        for tx in range(3):
            window = shifts[pl.ds(start + tx, 4)].reshape(256, 1152)
            piece = jnp.dot(
                window, taps[9 * tx : 9 * tx + 9].reshape(1152, 128),
                preferred_element_type=F32,
            )
            total = piece if total is None else total + piece
        planes = pl.ds(4 * part, 4)
        keep = mask[planes].reshape(256, 128) > 0.5
        out[planes] = jnp.where(keep, total, 0.0).astype(BF).reshape(4, 64, 128)

    def products(shifts, taps, out, lo, hi):
        def one(part, carry):
            product(shifts, taps, out, part)
            return carry

        lax.fori_loop(lo, hi, one, 0)

    cbuf[128 * 27 :, :] = jnp.zeros((SLOT, 128), F32)
    round_wait(0)
    round_signal(1)
    own_planes(xm, xs)
    for k in range(8):
        gt[:, 128 * k : 128 * k + 128] = gmb[2 * k : 2 * k + 2].reshape(128, 128).T
    kernel_grad(1)
    core_send(0)
    round_wait(1)
    round_signal(2)
    for side in range(2):
        halos[side][0].wait()
        halos[side][1].wait()
    rim_planes(halo_x, xs)
    kernel_grad(0)
    core_send(1)
    round_wait(2)
    xy_send(0)
    kernel_grad(2)
    core_send(2)
    xy_send(1)
    own_planes(gm, gs)
    loads[3].wait()
    products(xs, wv, resp_ref, 0, 1)
    xy_send(2)
    halos[0][2].wait()
    halos[1][2].wait()
    rim_planes(halo_g, gs)
    transposed_weights()
    products(xs, wv, resp_ref, 1, 3)
    z_send(0)
    z_send(1)
    z_send(2)
    products(xs, wv, resp_ref, 3, 4)
    products(gs, wt, gin_ref, 0, 3)

    def z_done(k, carry):
        source = lax.rem(me_z + k, 8)
        z_copy(source, source).wait_recv()
        z_copy(me_z, source).wait_send()
        return carry

    lax.fori_loop(1, 8, z_done, 0)
    rz[me_z] = zp[me_z]
    total = rz[0]
    for z in range(1, 8):
        total = total + rz[z]
    fin[me_y] = total * (1.0 / math.sqrt(4 * 128 * 8**3))

    def y_copy(slot, k):
        return pltpu.make_async_remote_copy(
            src_ref=fin.at[me_y],
            dst_ref=fin.at[slot],
            send_sem=y_s.at[k],
            recv_sem=y_r.at[slot],
            device_id=at(lax.rem(me_y + k, 4), me_z, me_x, me_c),
            device_id_type=MESH,
        )

    for k in range(1, 4):
        y_copy(me_y, k).start()
    products(gs, wt, gin_ref, 3, 4)
    for k in range(1, 4):
        y_copy(lax.rem(me_y + k, 4), k).wait_recv()
        y_copy(me_y, k).wait_send()
    for q in range(4):
        rows = min(PART, ROWS - PART * q)
        gw_ref[PART * q : PART * q + rows, :] = fin[q, :rows]


def store_kernel(a, b, c, a_out, b_out, c_out, sem):
    copies = [
        pltpu.make_async_copy(src, dst, sem.at[i])
        for i, (src, dst) in enumerate(((a, a_out), (b, b_out), (c, c_out)))
    ]
    for copy in copies:
        copy.start()
    for copy in copies:
        copy.wait()


def per_device(features, occupancy, neighbours, weight, cotangent):
    dma = pltpu.SemaphoreType.DMA
    anywhere = pl.BlockSpec(memory_space=pl.ANY)
    resp, gin, gw = pl.pallas_call(
        kernel,
        out_shape=(
            pltpu.VMEM((16, 64, 128), BF),
            pltpu.VMEM((16, 64, 128), BF),
            pltpu.VMEM((ROWS, 128), F32),
        ),
        in_specs=[
            anywhere,
            anywhere,
            anywhere,
            pl.BlockSpec(memory_space=pltpu.SMEM),
            anywhere,
        ],
        out_specs=(pl.BlockSpec(memory_space=pltpu.VMEM),) * 3,
        scratch_shapes=[
            pltpu.VMEM((2, 8, 64, 128), BF),
            pltpu.VMEM((2, 8, 64, 128), BF),
            pltpu.VMEM((2, 8, 8, 8), jnp.int32),
            pltpu.VMEM((27, 128, 128), BF),
            pltpu.VMEM((27, 128, 128), BF),
            pltpu.VMEM((16, 64, 128), F32),
            pltpu.VMEM((16, 8, 8, 128), F32),
            pltpu.VMEM((16, 8, 8, 128), F32),
            pltpu.VMEM((16, 64, 128), BF),
            pltpu.VMEM((128, 1024), BF),
            pltpu.VMEM((20, 64, 1152), BF),
            pltpu.VMEM((20, 64, 1152), BF),
            pltpu.VMEM((2, 2, 64, 128), BF),
            pltpu.VMEM((2, 2, 64, 128), BF),
            pltpu.VMEM((2, 2, 8, 8), jnp.int32),
            pltpu.VMEM((3472, 128), F32),
            pltpu.VMEM((32, 4, SLOT, 128), F32),
            pltpu.VMEM((32, 4, SLOT, 128), F32),
            pltpu.VMEM((4, 4, 8, SLOT, 128), jnp.int16),
            pltpu.VMEM((8, SLOT, 128), F32),
            pltpu.VMEM((15, 8, SLOT, 128), jnp.int16),
            pltpu.VMEM((8, SLOT, 128), F32),
            pltpu.VMEM((8, SLOT, 128), F32),
            pltpu.VMEM((4, SLOT, 128), F32),
            dma((4,)),
            dma((3, 2)),
            dma((3, 2)),
            dma((3,)),
            dma((3,)),
            dma((3, 15)),
            dma((3, 15)),
            dma((8,)),
            dma((8,)),
            dma((4,)),
            dma((4,)),
            pltpu.SemaphoreType.REGULAR((3,)),
        ],
        compiler_params=pltpu.CompilerParams(collective_id=0, has_side_effects=True),
        name="sparse_conv_step",
    )(
        features.reshape(2, 8, 64, 128),
        cotangent.reshape(2, 8, 64, 128),
        occupancy[0],
        neighbours[0],
        weight,
    )
    in_vmem = pl.BlockSpec(memory_space=pltpu.VMEM)
    resp, gin, gw = pl.pallas_call(
        store_kernel,
        out_shape=tuple(jax.ShapeDtypeStruct(v.shape, v.dtype) for v in (resp, gin, gw)),
        in_specs=[in_vmem] * 3,
        out_specs=(anywhere,) * 3,
        scratch_shapes=[dma((3,))],
        name="store_results",
    )(*(pltpu.with_memory_space_constraint(v, pltpu.VMEM) for v in (resp, gin, gw)))
    shape = features.shape
    return resp.reshape(shape), gin.reshape(shape), gw


def solution(mesh):
    placed = (
        P("dp", "space", None, None, None, None),
        P("dp", "space", None, None, None),
        P("dp", "space", None),
        P(),
        P("dp", "space", None, None, None, None),
    )
    return jax.shard_map(
        per_device,
        mesh=mesh,
        in_specs=placed,
        out_specs=(
            P("dp", "space", None, None, None, None),
            P("dp", "space", None, None, None, None),
            P("space", None),
        ),
        check_vma=False,
    )
```

```python
import functools
import math

import jax
import jax.numpy as jnp
from jax import lax
from jax.experimental import pallas as pl
from jax.experimental.pallas import tpu as pltpu
from jax.sharding import PartitionSpec as P

MESH = pl.DeviceIdType.MESH
BF = jnp.bfloat16
F32 = jnp.float32
ROWS = 54
PART = 14
SLOT = 16
CHUNKS = ((3, 2), (0, 3), (5, 3))


def slot_of(dx, dy, dz):
    number = 9 * (dx + 1) + 3 * (dy + 1) + (dz + 1)
    return number if number < 13 else number - 1


def kernel(
    x_hbm, g_hbm, occ_hbm, links, w_hbm,
    resp_ref, gin_ref, gw_ref,
    xv, gv, occv, wv, wt, mask, xm, gm, gmb, gt, xs, gs,
    halo_x, halo_g, halo_o, cbuf, csnd, crcv, xyb, own, rxy, zp, rz, fin,
    in_sem, halo_s, halo_r, core_s, core_r, xy_s, xy_r, z_s, z_r, y_s, y_r, ready,
):
    me_y = lax.axis_index("dp")
    me_s = lax.axis_index("space")
    me_c = lax.rem(me_s, 2)
    me_x = lax.rem(me_s // 2, 4)
    me_z = me_s // 8
    other_c = 1 - me_c

    def at(y, z, x, c):
        return (y, (z * 4 + x) * 2 + c)

    after = (me_y, lax.rem(me_s + 1, 64))
    before = (me_y, lax.rem(me_s + 63, 64))
    partner = at(me_y, me_z, me_x, other_c)

    def xy_peer(k):
        return lax.rem(me_x + k // 4, 4), lax.rem(me_y + lax.rem(k, 4), 4)

    loads = [
        pltpu.make_async_copy(src, dst, in_sem.at[i])
        for i, (src, dst) in enumerate(
            ((occ_hbm, occv), (x_hbm, xv), (g_hbm, gv), (w_hbm, wv))
        )
    ]
    for load in loads:
        load.start()

    barrier = pltpu.get_barrier_semaphore()

    def greet(device):
        pl.semaphore_signal(barrier, inc=1, device_id=device, device_id_type=MESH)

    near = [
        at(me_y, me_z, lax.rem(me_x + d, 4), me_c) for d in (1, 3)
    ] + [
        at(lax.rem(me_y + d, 4), me_z, me_x, me_c) for d in (1, 3)
    ] + [
        at(me_y, lax.rem(me_z + d, 8), me_x, me_c) for d in (1, 7)
    ]
    for device in [before, after, partner] + near:
        greet(device)

    def round_signal(r):
        for device in near:
            pl.semaphore_signal(ready.at[r], inc=1, device_id=device, device_id_type=MESH)

    def round_wait(r):
        pl.semaphore_wait(ready.at[r], 6)

    for load in loads[:3]:
        load.wait()

    eye = (
        lax.broadcasted_iota(jnp.int32, (8, 8, 8), 1)
        == lax.broadcasted_iota(jnp.int32, (8, 8, 8), 2)
    )
    ones = jnp.ones((8, 128), F32)

    def mask_of(occ):
        spread = jnp.broadcast_to(occ[:, None, :], (8, 8, 8))
        picked = jnp.where(eye & (spread > 0), 1.0, 0.0).astype(F32).reshape(64, 8)
        return jnp.dot(picked, ones, preferred_element_type=F32)

    def mask_plane(i, carry):
        b, p = i // 8, lax.rem(i, 8)
        m = mask_of(occv[b, p])
        mask[i] = m
        keep = m > 0.5
        xk = jnp.where(keep, xv[b, p].astype(F32), 0.0)
        gk = jnp.where(keep, gv[b, p].astype(F32), 0.0)
        xm[i] = xk.reshape(8, 8, 128)
        gm[i] = gk.reshape(8, 8, 128)
        gmb[i] = gk.astype(BF)
        return carry

    lax.fori_loop(0, 16, mask_plane, 0, unroll=4)

    pl.semaphore_wait(barrier, 9)

    def halo_copies(side):
        plane = 7 * side
        return [
            pltpu.make_async_remote_copy(
                src_ref=src.at[:, plane],
                dst_ref=dst.at[1 - side],
                send_sem=halo_s.at[t, side],
                recv_sem=halo_r.at[t, 1 - side],
                device_id=after if side == 1 else before,
                device_id_type=MESH,
            )
            for t, (src, dst) in enumerate(
                ((occ_hbm, halo_o), (x_hbm, halo_x), (g_hbm, halo_g))
            )
        ]

    halos = [halo_copies(0), halo_copies(1)]
    for t in range(3):
        for side in range(2):
            halos[side][t].start()
    round_signal(0)


    zi = lax.broadcasted_iota(jnp.int32, (10, 8, 128), 1)

    def weights_of(b, dx, local):
        wanted = (me_s + dx) * 2 + local

        def one(dy, dz):
            link = links[b, slot_of(dx, dy, dz)]
            return jnp.where((link == wanted) & (link >= 0), 1.0, 0.0).astype(F32)

        return one

    def put_plane(dst, index, centre, low, high):
        shifted = (
            pltpu.roll(jnp.where(zi == 7, low, centre), 1, 1),
            centre,
            pltpu.roll(jnp.where(zi == 0, high, centre), 7, 1),
        )
        for ty in range(3):
            for tz in range(3):
                col = (3 * ty + tz) * 128
                dst[index, :, col : col + 128] = (
                    shifted[tz][ty : ty + 8].reshape(64, 128).astype(BF)
                )

    def own_planes(src, dst):
        for b in range(2):
            one = weights_of(b, 0, 1 - b)
            w = {
                (dy, dz): one(dy, dz)
                for dy in (-1, 0, 1)
                for dz in (-1, 0, 1)
                if (dy, dz) != (0, 0)
            }

            def plane(p, carry, b=b, w=w):
                mine = src[8 * b + p]
                theirs = src[8 * (1 - b) + p]
                first, last = theirs[0:1], theirs[7:8]

                def zone(dz):
                    middle = mine if dz == 0 else theirs * w[0, dz]
                    return jnp.concatenate(
                        [last * w[-1, dz], middle, first * w[1, dz]], axis=0
                    )

                put_plane(dst, 10 * b + p + 1, zone(0), zone(-1), zone(1))
                return carry

            lax.fori_loop(0, 8, plane, 0)

    def rim_planes(halo, dst):
        for side, dx in ((0, -1), (1, 1)):
            p0, p1 = (
                jnp.where(
                    mask_of(halo_o[side, b]) > 0.5, halo[side, b].astype(F32), 0.0
                ).reshape(8, 8, 128)
                for b in range(2)
            )
            for b in range(2):
                w0 = weights_of(b, dx, 0)
                w1 = weights_of(b, dx, 1)

                def zone(dz):
                    def mix(dy, rows):
                        return p0[rows] * w0(dy, dz) + p1[rows] * w1(dy, dz)

                    return jnp.concatenate(
                        [mix(-1, slice(7, 8)), mix(0, slice(0, 8)), mix(1, slice(0, 1))],
                        axis=0,
                    )

                put_plane(dst, 10 * b + 9 * side, zone(0), zone(-1), zone(1))

    def kernel_grad(tx):
        for ty in range(3):
            total = None
            for b in range(2):
                window = xs[10 * b + tx : 10 * b + tx + 8, :, 384 * ty : 384 * ty + 384]
                part = jnp.dot(
                    gt[:, 512 * b : 512 * b + 512],
                    window.reshape(512, 384),
                    preferred_element_type=F32,
                )
                total = part if total is None else total + part
            for tz in range(3):
                tap = 9 * tx + 3 * ty + tz
                cbuf[128 * tap : 128 * tap + 128, :] = total[:, 128 * tz : 128 * tz + 128].T

    def core_copy(n):
        z0, nz = CHUNKS[n]
        return pltpu.make_async_remote_copy(
            src_ref=csnd.at[pl.ds(4 * z0, 4 * nz)],
            dst_ref=crcv.at[pl.ds(4 * z0, 4 * nz)],
            send_sem=core_s.at[n],
            recv_sem=core_r.at[n],
            device_id=partner,
            device_id_type=MESH,
        )

    def core_send(n):
        z0, nz = CHUNKS[n]

        def fill(j, carry):
            for q in range(4):
                csnd[j, q] = cbuf[pl.ds(ROWS * (2 * j + other_c) + PART * q, SLOT), :]
            return carry

        lax.fori_loop(4 * z0, 4 * (z0 + nz), fill, 0, unroll=4)
        core_copy(n).start()

    row_of = lax.broadcasted_iota(jnp.int32, (SLOT, 128), 0)

    def coded(v):
        top = jnp.max(jnp.abs(v), axis=0, keepdims=True)
        power = jnp.ceil(jnp.log2(jnp.maximum(top, 2e-33) * (1.0 / 32000.0)))
        return (
            jnp.where(row_of == PART, power, jnp.round(v * jnp.exp2(-power)))
            .astype(jnp.int32)
            .astype(jnp.int16)
        )

    def decoded(c):
        v = c.astype(jnp.int32).astype(F32)
        return v * jnp.exp2(v[PART : PART + 1])

    def xy_copy(n, k):
        z0, nz = CHUNKS[n]
        px, py = xy_peer(k)
        return pltpu.make_async_remote_copy(
            src_ref=xyb.at[px, py, pl.ds(z0, nz)],
            dst_ref=rxy.at[k - 1, pl.ds(z0, nz)],
            send_sem=xy_s.at[n, k - 1],
            recv_sem=xy_r.at[n, k - 1],
            device_id=at(py, me_z, px, me_c),
            device_id_type=MESH,
        )

    def xy_send(n):
        z0, nz = CHUNKS[n]
        core_copy(n).wait()

        def fill(j, carry):
            for q in range(4):
                mine = cbuf[pl.ds(ROWS * (2 * j + me_c) + PART * q, SLOT), :]
                xyb[lax.rem(j, 4), q, j // 4] = coded(mine + crcv[j, q])
            return carry

        lax.fori_loop(4 * z0, 4 * (z0 + nz), fill, 0, unroll=4)

        def go(k, carry):
            xy_copy(n, k).start()
            return carry

        lax.fori_loop(1, 16, go, 0)

        def keep(z, carry):
            j = 4 * z + me_x
            own[z] = (
                cbuf[pl.ds(ROWS * (2 * j + me_c) + PART * me_y, SLOT), :]
                + crcv[j, me_y]
            )
            return carry

        lax.fori_loop(z0, z0 + nz, keep, 0)

    def z_copy(slot, target):
        return pltpu.make_async_remote_copy(
            src_ref=zp.at[target],
            dst_ref=rz.at[slot],
            send_sem=z_s.at[target],
            recv_sem=z_r.at[slot],
            device_id=at(me_y, target, me_x, me_c),
            device_id_type=MESH,
        )

    def z_send(n):
        z0, nz = CHUNKS[n]

        def arrived(k, carry):
            xy_copy(n, k).wait()
            return carry

        lax.fori_loop(1, 16, arrived, 0)

        def add(z, carry):
            total = own[z]
            for k in range(15):
                total = total + decoded(rxy[k, z])
            zp[z] = total
            return carry

        lax.fori_loop(z0, z0 + nz, add, 0, unroll=True)

        def send(z, carry):
            @pl.when(z != me_z)
            def _():
                z_copy(me_z, z).start()

            return carry

        lax.fori_loop(z0, z0 + nz, send, 0)

    def transposed_weights(lo, hi):
        def turn(t, carry):
            wt[26 - t] = wv[t].T
            return carry

        lax.fori_loop(lo, hi, turn, 0, unroll=3)

    def product(shifts, taps, out, part):
        b = part // 2
        start = 10 * b + 4 * lax.rem(part, 2)
        total = None
        for tx in range(3):
            window = shifts[pl.ds(start + tx, 4)].reshape(256, 1152)
            piece = jnp.dot(
                window, taps[9 * tx : 9 * tx + 9].reshape(1152, 128),
                preferred_element_type=F32,
            )
            total = piece if total is None else total + piece
        planes = pl.ds(4 * part, 4)
        keep = mask[planes].reshape(256, 128) > 0.5
        out[planes] = jnp.where(keep, total, 0.0).astype(BF).reshape(4, 64, 128)

    def products(shifts, taps, out, lo, hi):
        def one(part, carry):
            product(shifts, taps, out, part)
            return carry

        lax.fori_loop(lo, hi, one, 0)

    cbuf[128 * 27 :, :] = jnp.zeros((SLOT, 128), F32)
    round_wait(0)
    round_signal(1)
    own_planes(xm, xs)
    for k in range(8):
        gt[:, 128 * k : 128 * k + 128] = gmb[2 * k : 2 * k + 2].reshape(128, 128).T
    kernel_grad(1)
    core_send(0)
    round_wait(1)
    round_signal(2)
    loads[3].wait()
    transposed_weights(0, 9)
    for side in range(2):
        halos[side][0].wait()
        halos[side][1].wait()
    rim_planes(halo_x, xs)
    kernel_grad(0)
    core_send(1)
    round_wait(2)
    xy_send(0)
    kernel_grad(2)
    core_send(2)
    xy_send(1)
    own_planes(gm, gs)
    products(xs, wv, resp_ref, 0, 1)
    xy_send(2)
    halos[0][2].wait()
    halos[1][2].wait()
    rim_planes(halo_g, gs)
    transposed_weights(9, 27)
    products(xs, wv, resp_ref, 1, 3)
    z_send(0)
    z_send(1)
    z_send(2)
    products(xs, wv, resp_ref, 3, 4)
    products(gs, wt, gin_ref, 0, 2)

    def z_done(k, carry):
        source = lax.rem(me_z + k, 8)
        z_copy(source, source).wait_recv()
        z_copy(me_z, source).wait_send()
        return carry

    lax.fori_loop(1, 8, z_done, 0)
    rz[me_z] = zp[me_z]
    total = rz[0]
    for z in range(1, 8):
        total = total + rz[z]
    fin[me_y] = total * (1.0 / math.sqrt(4 * 128 * 8**3))

    def y_copy(slot, k):
        return pltpu.make_async_remote_copy(
            src_ref=fin.at[me_y],
            dst_ref=fin.at[slot],
            send_sem=y_s.at[k],
            recv_sem=y_r.at[slot],
            device_id=at(lax.rem(me_y + k, 4), me_z, me_x, me_c),
            device_id_type=MESH,
        )

    for k in range(1, 4):
        y_copy(me_y, k).start()
    products(gs, wt, gin_ref, 2, 4)
    for k in range(1, 4):
        y_copy(lax.rem(me_y + k, 4), k).wait_recv()
        y_copy(me_y, k).wait_send()
    for q in range(4):
        rows = min(PART, ROWS - PART * q)
        gw_ref[PART * q : PART * q + rows, :] = fin[q, :rows]


def store_kernel(a, b, c, a_out, b_out, c_out, sem):
    copies = [
        pltpu.make_async_copy(src, dst, sem.at[i])
        for i, (src, dst) in enumerate(((a, a_out), (b, b_out), (c, c_out)))
    ]
    for copy in copies:
        copy.start()
    for copy in copies:
        copy.wait()


def per_device(features, occupancy, neighbours, weight, cotangent):
    dma = pltpu.SemaphoreType.DMA
    anywhere = pl.BlockSpec(memory_space=pl.ANY)
    resp, gin, gw = pl.pallas_call(
        kernel,
        out_shape=(
            pltpu.VMEM((16, 64, 128), BF),
            pltpu.VMEM((16, 64, 128), BF),
            pltpu.VMEM((ROWS, 128), F32),
        ),
        in_specs=[
            anywhere,
            anywhere,
            anywhere,
            pl.BlockSpec(memory_space=pltpu.SMEM),
            anywhere,
        ],
        out_specs=(pl.BlockSpec(memory_space=pltpu.VMEM),) * 3,
        scratch_shapes=[
            pltpu.VMEM((2, 8, 64, 128), BF),
            pltpu.VMEM((2, 8, 64, 128), BF),
            pltpu.VMEM((2, 8, 8, 8), jnp.int32),
            pltpu.VMEM((27, 128, 128), BF),
            pltpu.VMEM((27, 128, 128), BF),
            pltpu.VMEM((16, 64, 128), F32),
            pltpu.VMEM((16, 8, 8, 128), F32),
            pltpu.VMEM((16, 8, 8, 128), F32),
            pltpu.VMEM((16, 64, 128), BF),
            pltpu.VMEM((128, 1024), BF),
            pltpu.VMEM((20, 64, 1152), BF),
            pltpu.VMEM((20, 64, 1152), BF),
            pltpu.VMEM((2, 2, 64, 128), BF),
            pltpu.VMEM((2, 2, 64, 128), BF),
            pltpu.VMEM((2, 2, 8, 8), jnp.int32),
            pltpu.VMEM((3472, 128), F32),
            pltpu.VMEM((32, 4, SLOT, 128), F32),
            pltpu.VMEM((32, 4, SLOT, 128), F32),
            pltpu.VMEM((4, 4, 8, SLOT, 128), jnp.int16),
            pltpu.VMEM((8, SLOT, 128), F32),
            pltpu.VMEM((15, 8, SLOT, 128), jnp.int16),
            pltpu.VMEM((8, SLOT, 128), F32),
            pltpu.VMEM((8, SLOT, 128), F32),
            pltpu.VMEM((4, SLOT, 128), F32),
            dma((4,)),
            dma((3, 2)),
            dma((3, 2)),
            dma((3,)),
            dma((3,)),
            dma((3, 15)),
            dma((3, 15)),
            dma((8,)),
            dma((8,)),
            dma((4,)),
            dma((4,)),
            pltpu.SemaphoreType.REGULAR((3,)),
        ],
        compiler_params=pltpu.CompilerParams(collective_id=0, has_side_effects=True),
        name="sparse_conv_step",
    )(
        features.reshape(2, 8, 64, 128),
        cotangent.reshape(2, 8, 64, 128),
        occupancy[0],
        neighbours[0],
        weight,
    )
    in_vmem = pl.BlockSpec(memory_space=pltpu.VMEM)
    resp, gin, gw = pl.pallas_call(
        store_kernel,
        out_shape=tuple(jax.ShapeDtypeStruct(v.shape, v.dtype) for v in (resp, gin, gw)),
        in_specs=[in_vmem] * 3,
        out_specs=(anywhere,) * 3,
        scratch_shapes=[dma((3,))],
        name="store_results",
    )(*(pltpu.with_memory_space_constraint(v, pltpu.VMEM) for v in (resp, gin, gw)))
    shape = features.shape
    return resp.reshape(shape), gin.reshape(shape), gw


def solution(mesh):
    placed = (
        P("dp", "space", None, None, None, None),
        P("dp", "space", None, None, None),
        P("dp", "space", None),
        P(),
        P("dp", "space", None, None, None, None),
    )
    return jax.shard_map(
        per_device,
        mesh=mesh,
        in_specs=placed,
        out_specs=(
            P("dp", "space", None, None, None, None),
            P("dp", "space", None, None, None, None),
            P("space", None),
        ),
        check_vma=False,
    )
```
